32 devices in a mesh: sup: 16 (over z, y, x), cls: 2 (over core).
Axes of the slice: x: 2, y: 2, z: 4, core: 2. Of those that a mesh axis runs over, the one named last changes fastest.
Arguments:
- support_feats: bfloat16 [512, 8192], P('sup', 'cls'), may hold values from -6 to 6
- target_feats: bfloat16 [128, 8192], P('sup', 'cls'), may hold values from -6 to 6
- scales: bfloat16 [512], replicated, may hold values from 0.5 to 2
- soft_labels: float32 [512, 5376], P('sup', 'cls'), may hold values from -6 to 6
- target_labels: int32 [128], P('sup'), may hold values from 0 to 5375
Outputs:
- predictions: bfloat16 [128, 5376], P('sup', 'cls')
- hypergrad: float32 [512, 5376], P('sup', 'cls')
The draws below stay inside these ranges and needn't reach their ends.
All inputs are finite; a program needn't handle non-finite values.
Results may differ from the reference program's by a relative error of at most 0.017.
Values may be sent and summed in bfloat16 or wider, within the bound.
No kernel may reach another device: no remote copies, remote signals or barrier semaphores. Data moves between devices by JAX's collectives and lax.ppermute only.
A program may use at most 64 MiB of HBM per device.

```python
import math
import jax
import jax.numpy as jnp
from jax import lax

F = 8192
ITERS = 2
C = 5376
NS = 512
NT = 128


def touch_ends(array, rng, low, top_value):
    index_at = [jax.random.randint(jax.random.fold_in(rng, axis), (), 0, length) for axis, length in enumerate(array.shape)]
    main_axis = array.shape.index(max(array.shape))
    next_to = index_at[:main_axis] + [(index_at[main_axis] + 1) % array.shape[main_axis]] + index_at[main_axis + 1:]
    return array.at[tuple(index_at)].set(low).at[tuple(next_to)].set(top_value)


def level_of(rng, dims, shards, least, high):
    level = 1.0
    for position, shards_of in shards:
        steps = jax.random.uniform(jax.random.fold_in(jax.random.fold_in(rng, 6), position), (shards_of,), jnp.float32, least / len(shards), high / len(shards))
        level = level * jnp.repeat(jnp.exp(steps), dims[position] // shards_of).reshape((-1,) + (1,) * (len(dims) - 1 - position))
    return level


def noise(rng, extent, deviation, limit, cuts=(), kind=jnp.bfloat16):
    values = deviation * jax.random.normal(rng, extent, jnp.float32)
    if cuts:
        values = values * level_of(rng, extent, cuts, -0.22, 0.18)
    return jnp.clip(values, -limit, limit).astype(kind)


def setup_inputs(seed: int = 0) -> dict:
    key_of = jax.random.split(jax.random.key(seed), 6)
    return {
        "support_feats": noise(key_of[0], (NS, F), 1.0, 6.0, ((0, 16), (1, 2))),
        "target_feats": noise(key_of[1], (NT, F), 1.0, 6.0, ((0, 16), (1, 2))),
        "scales": jnp.clip(jnp.exp(jax.random.uniform(key_of[2], (NS,), jnp.float32, math.log(0.5), math.log(2.0))), 0.5, 2.0).astype(jnp.bfloat16),
        "soft_labels": noise(key_of[3], (NS, C), 1.0, 6.0, ((0, 16), (1, 2)), jnp.float32),
        "target_labels": touch_ends(jax.random.randint(key_of[4], (NT,), 0, C), jax.random.fold_in(key_of[4], 1), 0, C - 1).astype(jnp.int32),
    }


RIDGE = 0.05
LABEL_SCALE = 16.0


def solve(kernel, rhs):
    result = jnp.zeros_like(rhs)
    resid = rhs
    direction = rhs
    norm_now = jnp.sum(resid * resid, axis=0)
    for step in range(ITERS):
        image = jnp.dot(kernel, direction.astype(jnp.bfloat16), preferred_element_type=jnp.float32)
        curve = jnp.sum(direction * image, axis=0)
        step_size = norm_now / curve
        result = result + step_size * direction
        resid = resid - step_size * image
        norm_next = jnp.sum(resid * resid, axis=0)
        direction = resid + (norm_next / norm_now) * direction
        norm_now = norm_next
    return result


def reference(support_feats, target_feats, scales, soft_labels, target_labels):
    scale_vec = scales.astype(jnp.float32)
    gram = jnp.dot(support_feats, support_feats.T, preferred_element_type=jnp.float32)
    support_kernel = (gram * (scale_vec[:, None] * scale_vec[None, :]) / F
                      + RIDGE * jnp.eye(NS, dtype=jnp.float32)).astype(jnp.bfloat16)
    alpha = solve(support_kernel, soft_labels)
    alpha_low = alpha.astype(jnp.bfloat16)
    cross_gram = jnp.dot(target_feats, support_feats.T, preferred_element_type=jnp.float32)
    cross_kernel = (cross_gram * scale_vec[None, :] / F).astype(jnp.bfloat16)
    predicted = jnp.dot(cross_kernel, alpha_low, preferred_element_type=jnp.float32)
    classes = jnp.arange(C, dtype=jnp.int32)
    onehot = (target_labels[:, None] == classes[None, :]).astype(jnp.float32)
    misfit = (predicted - LABEL_SCALE * onehot).astype(jnp.bfloat16)
    rhs = lax.dot_general(cross_kernel, misfit, (((0,), (0,)), ((), ())),
                          preferred_element_type=jnp.float32)
    hypergrad = solve(support_kernel, rhs)
    return predicted.astype(jnp.bfloat16), hypergrad
```

```python
import functools
import jax
import jax.numpy as jnp
from jax import lax
from jax.experimental import pallas as pl
from jax.experimental.pallas import tpu as pltpu
from jax.sharding import PartitionSpec as P

F = 8192
ITERS = 2


RIDGE = 0.05
LABEL_SCALE = 16.0
T = 128
f32 = jnp.float32
bf16 = jnp.bfloat16
VM = pl.BlockSpec(memory_space=pltpu.VMEM)
SM = pl.BlockSpec(memory_space=pltpu.SMEM)


def conjugate(rhs, kernel):
    resid = rhs
    direction = rhs
    result = None
    norm_now = jnp.sum(resid * resid, axis=0, keepdims=True)
    for step in range(ITERS):
        image = jnp.dot(kernel, direction.astype(bf16), preferred_element_type=f32)
        curve = jnp.sum(direction * image, axis=0, keepdims=True)
        step_size = norm_now / curve
        move = step_size * direction
        result = move if result is None else result + move
        if step + 1 < ITERS:
            resid = resid - step_size * image
            norm_next = jnp.sum(resid * resid, axis=0, keepdims=True)
            direction = resid + norm_next / norm_now * direction
            norm_now = norm_next
    return result


def plain(support_feats, target_feats, scales, soft_labels, target_labels):
    own_support = support_feats.shape[0]
    own_targets = target_feats.shape[0]
    class_count = soft_labels.shape[1]
    sup_count = lax.axis_size("sup")
    support_total = own_support * sup_count
    block_rows = own_targets + own_support
    scale_vec = scales.astype(f32)
    sup_index = lax.axis_index("sup")
    support_first = sup_index * own_support
    local_rows = jnp.concatenate([target_feats, support_feats], axis=0)
    partial_gram = lax.dot_general(
        local_rows,
        lax.all_gather(support_feats, "sup", axis=0, tiled=True),
        (((1,), (1,)), ((), ())),
        preferred_element_type=f32,
    )
    own_scales = lax.dynamic_slice_in_dim(scale_vec, support_first, own_support)
    factor_all = jnp.concatenate([jnp.ones((own_targets,), f32), own_scales])
    share = lax.psum_scatter(partial_gram, "cls", scatter_dimension=0, tiled=True)
    first_row = lax.axis_index("cls") * share.shape[0]
    count = share.shape[0]
    rows = first_row + lax.iota(jnp.int32, count)
    factor = lax.dynamic_slice_in_dim(factor_all, first_row, count)
    support_index = support_first + rows - own_targets
    on_diag = (lax.iota(jnp.int32, support_total)[None, :] == support_index[:, None]) & (
        rows >= own_targets
    )[:, None]
    scaled = share * (factor[:, None] * scale_vec[None, :]) / F
    finished = (scaled + jnp.where(on_diag, RIDGE, 0.0)).astype(bf16)
    kernels = lax.all_gather(finished, ("sup", "cls"), axis=0, tiled=True)
    blocks = kernels.reshape(sup_count, block_rows, support_total)
    cross_kernel = blocks[:, :own_targets].reshape(sup_count * own_targets, support_total)
    support_kernel = blocks[:, own_targets:].reshape(support_total, support_total)
    label_cols = lax.all_to_all(soft_labels, "sup", split_axis=1, concat_axis=0, tiled=True)
    col_width = label_cols.shape[1]
    labels_all = lax.all_gather(target_labels, "sup", axis=0, tiled=True)
    columns = (
        lax.axis_index("cls") * class_count + sup_index * col_width + lax.iota(jnp.int32, col_width)
    )
    alpha = conjugate(label_cols, support_kernel)
    predicted = jnp.dot(cross_kernel, alpha.astype(bf16), preferred_element_type=f32)
    onehot = (labels_all[:, None] == columns[None, :]).astype(f32)
    misfit = (predicted - LABEL_SCALE * onehot).astype(bf16)
    rhs = lax.dot_general(
        cross_kernel, misfit, (((0,), (0,)), ((), ())), preferred_element_type=f32
    )
    hyper_cols = conjugate(rhs, support_kernel)
    predictions = lax.all_to_all(
        predicted.astype(bf16), "sup", split_axis=0, concat_axis=1, tiled=True
    )
    hypergrad = lax.all_to_all(hyper_cols, "sup", split_axis=0, concat_axis=1, tiled=True)
    return (predictions, hypergrad)


def halves(blocks):
    cols = [[(i, j) for i in range(j, blocks + 1)] for j in range(blocks)]
    first, second = [], []
    for j, col in enumerate(cols):
        (first if j % 4 in (0, 3) else second).extend(col)
    return first, second


def pack_labels(ns, x_ref, t_ref, o_ref):
    own = x_ref.shape[0]
    rem = x_ref.shape[1] // ns - T
    half = own // 2
    for s in range(ns):
        o_ref[s, 0:own, :] = x_ref[:, s * T : (s + 1) * T]
        a = ns * T + s * rem
        o_ref[s, own : own + half, 0:rem] = x_ref[0:half, a : a + rem]
        o_ref[s, own : own + half, rem : 2 * rem] = x_ref[half:own, a : a + rem]
        o_ref[s, own : own + half, 2 * rem : T] = t_ref[:, 2 * rem : T]


def gram(ns, own_support, c_ref, a_ref, b_ref, o_ref, x_ref):
    width = a_ref.shape[2]
    total = ns * own_support
    for s in range(ns):
        r = slice(s * own_support, (s + 1) * own_support)
        x_ref[r, 0:width] = a_ref[s, 0:own_support]
        x_ref[r, width : 2 * width] = b_ref[s, 0:own_support]
    tgt = a_ref.shape[1] - own_support
    nt = ns * tgt
    x_ref[total : total + nt, 0:width] = a_ref[:, own_support:, :].reshape(nt, width)
    x_ref[total : total + nt, width : 2 * width] = b_ref[:, own_support:, :].reshape(nt, width)
    blocks = total // T
    rows_all = total + nt
    for half in range(2):
        @pl.when(c_ref[0] == half)
        def _():
            off = 0
            for j in range(blocks):
                if (j % 4 in (0, 3)) != (half == 0):
                    continue
                n = rows_all - j * T
                o_ref[off : off + n, :] = lax.dot_general(
                    x_ref[j * T :, :],
                    x_ref[j * T : (j + 1) * T, :],
                    (((1,), (1,)), ((), ())),
                    preferred_element_type=f32,
                )
                off += n


def finish(ns, p_ref, f_ref, d_ref, o_ref):
    total = p_ref[0]
    for s in range(1, ns):
        total = total + p_ref[s]
    done = (total * f_ref[...] + d_ref[...]).astype(bf16)
    for s in range(ns):
        o_ref[s] = done


def solve(ns, own, tgt, rem, c_ref, own_ref, oth_ref, lab_ref, o_ref, k_ref, g_ref):
    total = ns * own
    nt = ns * tgt
    blocks = total // T
    tables = halves(blocks)
    core = c_ref[0]
    for half in range(2):
        @pl.when(core == half)
        def _():
            for ref, table in ((own_ref, tables[half]), (oth_ref, tables[1 - half])):
                for m, (i, j) in enumerate(table):
                    block = ref[m * T : (m + 1) * T, :]
                    cols = slice(j * T, (j + 1) * T)
                    if i == blocks:
                        g_ref[:, cols] = block
                    else:
                        rows = slice(i * T, (i + 1) * T)
                        k_ref[rows, cols] = block
                        if i != j:
                            k_ref[cols, rows] = block.T
    half = own // 2
    main = lab_ref[:, 0:own, :].reshape(total, T)
    spill = lab_ref[:, own : own + half, :]
    moved = pltpu.roll(spill.reshape(ns * half, T), T - rem, 1).reshape(ns, half, T)
    extra = jnp.concatenate([spill, moved], axis=1).reshape(total, T)
    b = jnp.concatenate([main, extra], axis=1)
    kernel = k_ref[...]
    cross = g_ref[...]
    alpha = conjugate(b, kernel)
    predicted = jnp.dot(cross, alpha.astype(bf16), preferred_element_type=f32)
    lane = lax.broadcasted_iota(jnp.int32, (nt, 2 * T), 1)
    columns = jnp.where(lane < T, lane + c_ref[1], lane + c_ref[2]).astype(f32)
    classes = lab_ref[:, own : own + tgt, T - 1 : T].reshape(nt, 1)
    onehot = jnp.where(columns == classes, LABEL_SCALE, 0.0)
    misfit = (predicted - onehot).astype(bf16)
    rhs = lax.dot_general(cross, misfit, (((0,), (0,)), ((), ())), preferred_element_type=f32)
    hyper = conjugate(rhs, kernel).astype(bf16)
    low = predicted.astype(bf16)
    o_ref[:, 0:own, :] = hyper[:, 0:T].reshape(ns, own, T)
    o_ref[:, own : own + tgt, :] = low[:, 0:T].reshape(ns, tgt, T)
    tail = hyper[:, T : T + rem].reshape(ns, own, rem)
    o_ref[:, own + tgt :, 0:rem] = tail[:, 0:half]
    o_ref[:, own + tgt :, rem : 2 * rem] = tail[:, half:own]
    o_ref[:, own + tgt : own + 2 * tgt, 2 * rem : 3 * rem] = low[:, T : T + rem].reshape(ns, tgt, rem)


def unpack(ns, own, tgt, rem, x_ref, p_ref, h_ref):
    half = own // 2
    for s in range(ns):
        cols = slice(s * T, (s + 1) * T)
        h_ref[:, cols] = x_ref[s, 0:own].astype(f32)
        p_ref[:, cols] = x_ref[s, own : own + tgt]
        a = ns * T + s * rem
        tail = x_ref[s, own + tgt :].astype(f32)
        h_ref[0:half, a : a + rem] = tail[:, 0:rem]
        h_ref[half:own, a : a + rem] = tail[:, rem : 2 * rem]
        p_ref[:, a : a + rem] = tail[0:tgt, 2 * rem : 3 * rem].astype(bf16)


def packed(support_feats, target_feats, scales, soft_labels, target_labels):
    own, width = support_feats.shape
    tgt = target_feats.shape[0]
    ns = lax.axis_size("sup")
    total = own * ns
    blocks = total // T
    class_count = soft_labels.shape[1]
    rem = class_count // ns - T
    sup = lax.axis_index("sup")
    core = lax.axis_index("cls")
    scale_vec = scales.astype(f32)
    fb = width // ns

    rows = jnp.concatenate([support_feats, target_feats], axis=0)
    feats = rows.reshape(own + tgt, ns, fb).transpose(1, 0, 2)
    feats = lax.all_to_all(feats, "sup", 0, 0)

    half = own // 2
    classes = jnp.pad(target_labels.astype(f32), (0, half - tgt))
    classes = jnp.broadcast_to(classes[:, None], (half, T))
    labels = pl.pallas_call(
        functools.partial(pack_labels, ns),
        out_shape=jax.ShapeDtypeStruct((ns, own + half, T), f32),
        in_specs=[VM, VM],
        out_specs=VM,
    )(soft_labels, classes)
    labels = lax.all_to_all(labels, "sup", 0, 0)

    first, second = halves(blocks)
    count = len(first) * T
    chunk = count // ns
    by_block = scale_vec.reshape(blocks, T)
    row_scale = jnp.concatenate([by_block, jnp.ones((1, T), f32)])
    order = first + second
    left = jnp.concatenate([row_scale[i] for i, _ in order])
    mine = core * count + sup * chunk
    left = lax.dynamic_slice_in_dim(left, mine, chunk)
    spot = mine + lax.iota(jnp.int32, chunk)
    which = spot // T
    right = jnp.stack([by_block[j] for _, j in order])
    right = right[which]
    factor = left[:, None] * right / F
    on_diag = jnp.array([i == j for i, j in order])[which]
    diag = jnp.where(
        on_diag[:, None] & (lax.iota(jnp.int32, T)[None, :] == (spot % T)[:, None]), RIDGE, 0.0
    ).astype(f32)

    swap = [(0, 1), (1, 0)]
    other = lax.ppermute(feats, "cls", swap)
    info = jnp.stack(
        [core, core * class_count + sup * T, core * class_count + ns * T + sup * rem - T]
    ).astype(jnp.int32)
    partial = pl.pallas_call(
        functools.partial(gram, ns, own),
        out_shape=jax.ShapeDtypeStruct((count, T), f32),
        in_specs=[SM, VM, VM],
        out_specs=VM,
        scratch_shapes=[pltpu.VMEM((total + ns * tgt, 2 * fb), bf16)],
    )(info, feats, other)
    partial = lax.all_to_all(partial.reshape(ns, chunk, T), "sup", 0, 0)
    done = pl.pallas_call(
        functools.partial(finish, ns),
        out_shape=jax.ShapeDtypeStruct((ns, chunk, T), bf16),
        in_specs=[VM, VM, VM],
        out_specs=VM,
    )(partial, factor, diag)
    done = lax.all_to_all(done, "sup", 0, 0).reshape(count, T)
    done_other = lax.ppermute(done, "cls", swap)
    result = pl.pallas_call(
        functools.partial(solve, ns, own, tgt, rem),
        out_shape=jax.ShapeDtypeStruct((ns, own + tgt + half, T), bf16),
        in_specs=[SM, VM, VM, VM],
        out_specs=VM,
        scratch_shapes=[pltpu.VMEM((total, total), bf16), pltpu.VMEM((ns * tgt, total), bf16)],
    )(info, done, done_other, labels)
    result = lax.all_to_all(result, "sup", 0, 0)
    return tuple(
        pl.pallas_call(
            functools.partial(unpack, ns, own, tgt, rem),
            out_shape=(
                jax.ShapeDtypeStruct((tgt, class_count), bf16),
                jax.ShapeDtypeStruct((own, class_count), f32),
            ),
            in_specs=[VM],
            out_specs=(VM, VM),
        )(result)
    )


def fits(mesh, args):
    ns, nc = mesh.shape["sup"], mesh.shape["cls"]
    total, feats = args[0].shape
    nt = args[1].shape[0]
    classes = args[3].shape[1]
    if nc != 2 or total % T or nt != T or (total // T) % 4 or total % (32 * ns):
        return False
    own, tgt, width = total // ns, nt // ns, classes // (nc * ns)
    first, second = halves(total // T)
    return (
        own == 32
        and tgt == 8
        and len(first) == len(second)
        and len(first) * T % (8 * ns) == 0
        and feats % (nc * ns * T) == 0
        and T < width <= T + T // 3
        and width % 8 == 0
    )


def solution(mesh):
    in_specs = (P("sup", "cls"), P("sup", "cls"), P(), P("sup", "cls"), P("sup"))
    out_specs = (P("sup", "cls"), P("sup", "cls"))

    def run(*args):
        body = packed if fits(mesh, args) else plain
        return jax.shard_map(
            body, mesh=mesh, in_specs=in_specs, out_specs=out_specs, check_vma=False
        )(*args)

    return run
```
